32 devices in a mesh: dp: 8 (over z, core), tensor: 4 (over y, x).
Axes of the slice: x: 2, y: 2, z: 4, core: 2. Of those that a mesh axis runs over, the one named last changes fastest.
Arguments:
- tokens: bfloat16 [12288, 2048], P(('dp', 'tensor')), may hold values from -6 to 6
- cotangent: bfloat16 [12288, 2048], P(('dp', 'tensor')), may hold values from -6 to 6
- prompt_len: int32 [4], replicated, may hold values from 512 to 1024, as said below
- cont_len: int32 [4, 8], P(None, 'dp'), may hold values from 1 to 256, as said below
- w_query: bfloat16 [2048, 2048], P('dp', 'tensor'), may hold values from -0.5 to 0.5
- key_weight: bfloat16 [2048, 512], P('dp', 'tensor'), may hold values from -0.5 to 0.5
- value_weight: bfloat16 [2048, 512], P('dp', 'tensor'), may hold values from -0.125 to 0.125
- w_out: bfloat16 [2048, 2048], P('tensor', 'dp'), may hold values from -2 to 2
- w_gate: bfloat16 [2048, 8192], P('dp', 'tensor'), may hold values from -0.125 to 0.125
- w_up: bfloat16 [2048, 8192], P('dp', 'tensor'), may hold values from -0.125 to 0.125
- w_down: bfloat16 [8192, 2048], P('tensor', 'dp'), may hold values from -0.5 to 0.5
- attn_gain: bfloat16 [2048], P('dp'), may hold values from 0.5 to 1.5
- ffn_gain: bfloat16 [2048], P('dp'), may hold values from 0.5 to 1.5
Outputs:
- output: bfloat16 [12288, 2048], P(('dp', 'tensor'))
- input_grad: float32 [12288, 2048], P(('dp', 'tensor'))
- grad_query: float32 [2048, 2048], P('dp', 'tensor')
- grad_key: float32 [2048, 512], P('dp', 'tensor')
- grad_value: float32 [2048, 512], P('dp', 'tensor')
- grad_out: float32 [2048, 2048], P('tensor', 'dp')
- grad_gate: float32 [2048, 8192], P('dp', 'tensor')
- grad_up: float32 [2048, 8192], P('dp', 'tensor')
- grad_down: float32 [8192, 2048], P('tensor', 'dp')
- grad_attn_gain: float32 [2048], P(('dp', 'tensor'))
- grad_ffn_gain: float32 [2048], P(('dp', 'tensor'))
The draws below stay inside these ranges and needn't reach their ends.
Inputs may be any that keep to these rules, and one draw needn't show every extreme that they name: `prompt_len`: prompt slots of a group beyond its length are padding; some group has exactly 1024 prompt tokens. `cont_len`: slots of a continuation beyond its length are padding; in each group some continuation has exactly 256 tokens.
All inputs are finite; a program needn't handle non-finite values.
Results may differ from the reference program's by a relative error of at most 0.024.
Values may be sent and summed in bfloat16 or wider, within the bound.
No kernel may reach another device: no remote copies, remote signals or barrier semaphores. Data moves between devices by JAX's collectives and lax.ppermute only.
A program may use at most 256 MiB of HBM per device.

```python
import jax
import jax.numpy as jnp
from jax import lax

MODEL_WIDTH = 2048
HQ = 32
KEY_VALUE_HEADS = 8
HEAD_SIZE = 64
FF = 8192
NG = 4
PROMPT_DEV = 128
CONT = 256
PROMPT = 1024
TOKENS = 12288
N_DP = 8


def draw_prompt_len(key, part):
    lengths = jax.random.randint(jax.random.fold_in(key, 11), (NG,), PROMPT // 2, PROMPT + 1)
    chosen = jax.random.randint(jax.random.fold_in(key, 12), (), 0, NG)
    return jnp.where(jnp.arange(NG) == chosen, PROMPT, lengths).astype(jnp.int32)


def draw_cont_len(key, part):
    lengths = jax.random.randint(jax.random.fold_in(key, 21), (NG, N_DP), 1, CONT + 1)
    chosen = jax.random.randint(jax.random.fold_in(key, 22), (NG,), 0, N_DP)
    return jnp.where(jnp.arange(N_DP)[None, :] == chosen[:, None], CONT, lengths).astype(jnp.int32)


def block_scale(rng, dims, pieces, least, top_value):
    gain, own = 1.0, jax.random.fold_in(rng, 6)
    for position, parts in pieces:
        steps = jnp.exp(jax.random.uniform(jax.random.fold_in(own, position), (parts,), jnp.float32, least / len(pieces), top_value / len(pieces)))
        gain = gain * jnp.repeat(steps, dims[position] // parts).reshape([-1 if axis == position else 1 for axis in range(len(dims))])
    return gain


def gaussian(stream_key, extent, spread, most, pieces=(), held_as=jnp.bfloat16):
    drawn = spread * jax.random.normal(stream_key, extent, jnp.float32)
    if pieces:
        drawn = drawn * block_scale(stream_key, extent, pieces, -0.22, 0.18)
    return jnp.clip(drawn, -most, most).astype(held_as)


def setup_inputs(seed: int = 0) -> dict:
    key_list = jax.random.split(jax.random.key(seed), 14)
    tokens = gaussian(key_list[0], (TOKENS, MODEL_WIDTH), 1.0, 6.0, ((0, 32),))
    cotangent = gaussian(key_list[1], (TOKENS, MODEL_WIDTH), 1.0, 6.0, ((0, 32),))
    prompt_len = draw_prompt_len(jax.random.fold_in(key_list[13], 71), 0)
    cont_len = draw_cont_len(jax.random.fold_in(key_list[13], 71), 0)
    w_query = gaussian(key_list[4], (MODEL_WIDTH, HQ * HEAD_SIZE), (MODEL_WIDTH // 16) ** -0.5, 0.5, ((0, 8), (1, 4)))
    key_weight = gaussian(key_list[5], (MODEL_WIDTH, KEY_VALUE_HEADS * HEAD_SIZE), (MODEL_WIDTH // 16) ** -0.5, 0.5, ((0, 8), (1, 4)))
    value_weight = gaussian(key_list[6], (MODEL_WIDTH, KEY_VALUE_HEADS * HEAD_SIZE), MODEL_WIDTH ** -0.5, 0.125, ((0, 8), (1, 4)))
    w_out = gaussian(key_list[7], (HQ * HEAD_SIZE, MODEL_WIDTH), 8 ** -0.5, 2.0, ((0, 4), (1, 8)))
    w_gate = gaussian(key_list[8], (MODEL_WIDTH, FF), MODEL_WIDTH ** -0.5, 0.125, ((0, 8), (1, 4)))
    w_up = gaussian(key_list[9], (MODEL_WIDTH, FF), MODEL_WIDTH ** -0.5, 0.125, ((0, 8), (1, 4)))
    w_down = gaussian(key_list[10], (FF, MODEL_WIDTH), (FF // 64) ** -0.5, 0.5, ((0, 4), (1, 8)))
    attn_gain = jnp.clip(1.0 + 0.1 * jax.random.normal(key_list[11], (MODEL_WIDTH,), jnp.float32), 0.5, 1.5).astype(jnp.bfloat16)
    ffn_gain = jnp.clip(1.0 + 0.1 * jax.random.normal(key_list[12], (MODEL_WIDTH,), jnp.float32), 0.5, 1.5).astype(jnp.bfloat16)
    return {"tokens": tokens, "cotangent": cotangent, "prompt_len": prompt_len, "cont_len": cont_len, "w_query": w_query, "key_weight": key_weight, "value_weight": value_weight, "w_out": w_out, "w_gate": w_gate, "w_up": w_up, "w_down": w_down, "attn_gain": attn_gain, "ffn_gain": ffn_gain}


EPS = 1e-05
THETA = 10000000.0
ATTN_SCALE = 0.015625
RESID_SCALE = 0.22
NEG_FILL = -1e+30
HIGH_PRECISION = lax.Precision.HIGHEST

@jax.custom_vjp
def lower_precision(v):
    return lax.optimization_barrier(v.astype(jnp.bfloat16)).astype(jnp.float32)

@jax.custom_vjp
def low_back(v):
    return v

def low_keep(v):
    return (lower_precision(v), None)

def low_pass(kept, grad):
    return (grad,)

def back_keep(v):
    return (v, None)

def back_low(kept, grad):
    return (lower_precision(grad),)
lower_precision.defvjp(low_keep, low_pass)
low_back.defvjp(back_keep, back_low)

def matmul(left_mat, right_mat):
    return jnp.dot(left_mat, right_mat, precision=HIGH_PRECISION, preferred_element_type=jnp.float32)

def rms_norm(values, gain_vec):
    row_scale = lax.rsqrt(lax.optimization_barrier(jnp.mean(values * values, axis=-1, keepdims=True)) + EPS)
    return values * row_scale * gain_vec

def rope_tables(positions, head_width):
    half_width = head_width // 2
    frequency = THETA ** (-(jnp.arange(half_width).astype(jnp.float32) * 2.0) / head_width)
    angles = positions.astype(jnp.float32)[:, None] * frequency[None, :]
    angles = jnp.concatenate([angles, angles], axis=1)
    return (jnp.cos(angles), jnp.sin(angles))

def apply_rotary(values, cosine_table, sine_values):
    half_width = values.shape[-1] // 2
    turned = jnp.concatenate([-values[..., half_width:], values[..., :half_width]], axis=-1)
    return values * cosine_table[:, None, :] + turned * sine_values[:, None, :]

def build_mask(base_row, prompt_length, portion_rows, cont_rows, prompt_row_count):
    row_ids = jnp.arange(portion_rows + cont_rows).astype(jnp.int32)[:, None]
    key_ids = jnp.arange(prompt_row_count + cont_rows).astype(jnp.int32)[None, :]
    in_prompt = key_ids < prompt_row_count
    prompt_part = in_prompt & (key_ids <= base_row + row_ids)
    cont_part = jnp.where(in_prompt, key_ids < prompt_length, key_ids - prompt_row_count <= row_ids - portion_rows)
    return jnp.where(row_ids < portion_rows, prompt_part, cont_part)

def attend_ref(query_rows, key_row_set, value_row_set, key_mask):
    row_count, head_count, head_width = query_rows.shape
    group_count = key_row_set.shape[1]
    grouped_rows = query_rows.reshape(row_count, group_count, head_count // group_count, head_width)
    score_matrix = jnp.einsum('wclz,icz->clwi', grouped_rows, key_row_set, precision=HIGH_PRECISION)
    score_matrix = low_back(score_matrix * ATTN_SCALE)
    score_matrix = jnp.where(key_mask[None, None], score_matrix, NEG_FILL)
    row_top = lax.optimization_barrier(jnp.max(score_matrix, axis=-1, keepdims=True))
    weights = jnp.exp(score_matrix - row_top)
    probability_rows = lower_precision(weights / lax.optimization_barrier(jnp.sum(weights, axis=-1, keepdims=True)))
    merged_heads = jnp.einsum('yxks,syt->kyxt', probability_rows, value_row_set, precision=HIGH_PRECISION)
    return merged_heads.reshape(row_count, head_count * head_width)

def group_layer(x_group, prompt_length, weight_list):
    w_query, key_weight, value_weight, w_out, w_gate, w_up, w_down, attn_gain, ffn_gain = weight_list
    portion_rows = PROMPT_DEV
    block_row_set = PROMPT_DEV + CONT
    prompt_row_count = PROMPT_DEV * N_DP
    rows_all = x_group.reshape(N_DP * block_row_set, MODEL_WIDTH)
    normed = lower_precision(rms_norm(rows_all, attn_gain))
    query_proj = low_back(matmul(normed, w_query))
    key_projected = low_back(matmul(normed, key_weight))
    value_projected = lower_precision(low_back(matmul(normed, value_weight)))
    dev_ids = jnp.arange(N_DP).astype(jnp.int32)[:, None]
    col_ids = jnp.arange(block_row_set).astype(jnp.int32)[None, :]
    positions = jnp.where(col_ids < portion_rows, dev_ids * portion_rows + col_ids, prompt_length + col_ids - portion_rows).reshape(-1)
    cosine_table, sine_values = rope_tables(positions, HEAD_SIZE)
    query_rot = lower_precision(apply_rotary(query_proj.reshape(-1, HQ, HEAD_SIZE), cosine_table, sine_values)).reshape(N_DP, block_row_set, HQ, HEAD_SIZE)
    key_rotated = lower_precision(apply_rotary(key_projected.reshape(-1, KEY_VALUE_HEADS, HEAD_SIZE), cosine_table, sine_values)).reshape(N_DP, block_row_set, KEY_VALUE_HEADS, HEAD_SIZE)
    value_row_set = value_projected.reshape(N_DP, block_row_set, KEY_VALUE_HEADS, HEAD_SIZE)
    prompt_key_rows = key_rotated[:, :portion_rows].reshape(prompt_row_count, KEY_VALUE_HEADS, HEAD_SIZE)
    prompt_value_rows = value_row_set[:, :portion_rows].reshape(prompt_row_count, KEY_VALUE_HEADS, HEAD_SIZE)

    def one_piece(piece_items):
        query_piece, key_cont, val_cont, device = piece_items
        key_mask = build_mask(device * portion_rows, prompt_length, portion_rows, CONT, prompt_row_count)
        every_key = jnp.concatenate([prompt_key_rows, key_cont], axis=0)
        val_all = jnp.concatenate([prompt_value_rows, val_cont], axis=0)
        return attend_ref(query_piece, every_key, val_all, key_mask)
    merged_heads = lax.map(jax.checkpoint(one_piece), (query_rot, key_rotated[:, portion_rows:], value_row_set[:, portion_rows:], jnp.arange(N_DP).astype(jnp.int32)))
    merged_heads = low_back(lower_precision(merged_heads.reshape(N_DP * block_row_set, HQ * HEAD_SIZE)))
    attn_out = low_back(matmul(merged_heads, w_out))
    hidden = rows_all + RESID_SCALE * attn_out
    normed_two = lower_precision(rms_norm(hidden, ffn_gain))
    gate_val = low_back(matmul(normed_two, w_gate))
    up_val = low_back(matmul(normed_two, w_up))
    product = lower_precision(jax.nn.silu(gate_val) * up_val)
    ffn_out = low_back(matmul(product, w_down))
    return (hidden + RESID_SCALE * ffn_out).reshape(N_DP, block_row_set, MODEL_WIDTH)

def reference(tokens, cotangent, prompt_len, cont_len, w_query, key_weight, value_weight, w_out, w_gate, w_up, w_down, attn_gain, ffn_gain):
    block_row_set = PROMPT_DEV + CONT
    weights = tuple((item.astype(jnp.float32) for item in (w_query, key_weight, value_weight, w_out, w_gate, w_up, w_down, attn_gain, ffn_gain)))

    def forward(x_all, *weight_list):
        grouped_rows = x_all.reshape(N_DP, NG, block_row_set, MODEL_WIDTH).transpose(1, 0, 2, 3)

        def one_group(group_items):
            return group_layer(group_items[0], group_items[1], weight_list)
        result = lax.map(jax.checkpoint(one_group), (grouped_rows, prompt_len))
        return result.transpose(1, 0, 2, 3).reshape(N_DP * NG * block_row_set, MODEL_WIDTH)
    output, pull = jax.vjp(forward, tokens.astype(jnp.float32), *weights)
    col_ids = jnp.arange(block_row_set).astype(jnp.int32)[None, None, :]
    dev_ids = jnp.arange(N_DP).astype(jnp.int32)[:, None, None]
    valid_rows = jnp.where(col_ids < PROMPT_DEV, dev_ids * PROMPT_DEV + col_ids < prompt_len[None, :, None], col_ids - PROMPT_DEV < cont_len.T[:, :, None])
    masked_cotangent = cotangent.astype(jnp.float32) * valid_rows.reshape(-1, 1).astype(jnp.float32)
    grads = pull(masked_cotangent)
    return (output.astype(jnp.bfloat16), grads[0], grads[1], grads[2], grads[3], grads[4], grads[5], grads[6], grads[7], grads[8], grads[9])
```

```python
import jax
import jax.numpy as jnp
from jax import lax
from jax.sharding import PartitionSpec as P

HEAD_SIZE = 64
NG = 4
PROMPT_DEV = 128
CONT = 256


EPS = 1e-05
THETA = 10000000.0
ATTN_SCALE = 0.015625
RESID_SCALE = 0.22
NEG_FILL = -1e30


def project(left_mat, right_mat):
    return jnp.dot(left_mat, right_mat, preferred_element_type=jnp.float32)


def dot_rows(left_mat, right_mat):
    return lax.dot_general(
        left_mat, right_mat, (((0,), (0,)), ((), ())), preferred_element_type=jnp.float32
    )


def dot_back(left_mat, right_mat):
    return lax.dot_general(
        left_mat, right_mat, (((1,), (1,)), ((), ())), preferred_element_type=jnp.float32
    )


def rope_tables(positions, head_width):
    half_width = head_width // 2
    frequency = THETA ** (-(jnp.arange(half_width).astype(jnp.float32) * 2.0) / head_width)
    angles = positions.astype(jnp.float32)[:, None] * frequency[None, :]
    angles = jnp.concatenate([angles, angles], axis=1)
    return (jnp.cos(angles), jnp.sin(angles))


def apply_rotary(values, cosine_table, sine_values):
    half_width = values.shape[-1] // 2
    turned = jnp.concatenate([-values[..., half_width:], values[..., :half_width]], axis=-1)
    return values * cosine_table[:, None, :] + turned * sine_values[:, None, :]


def unrotate(values, cosine_table, sine_values):
    half_width = values.shape[-1] // 2
    scaled_sin = values * sine_values[:, None, :]
    turned = jnp.concatenate([scaled_sin[..., half_width:], -scaled_sin[..., :half_width]], axis=-1)
    return values * cosine_table[:, None, :] + turned


def build_mask(base_row, prompt_length, portion_rows, cont_rows, prompt_row_count):
    row_ids = jnp.arange(portion_rows + cont_rows)[:, None]
    key_ids = jnp.arange(prompt_row_count + cont_rows)[None, :]
    in_prompt = key_ids < prompt_row_count
    prompt_part = in_prompt & (key_ids <= base_row + row_ids)
    cont_part = jnp.where(
        in_prompt, key_ids < prompt_length, key_ids - prompt_row_count <= row_ids - portion_rows
    )
    return jnp.where(row_ids < portion_rows, prompt_part, cont_part)


def norm_parts(values):
    row_scale = lax.rsqrt(jnp.mean(values * values, axis=-1, keepdims=True) + EPS)
    return (values * row_scale, row_scale)


def norm_back(grad_norm, unit_rows, row_scale, gain_vec):
    scaled = grad_norm * gain_vec
    grad_in = row_scale * (
        scaled - unit_rows * jnp.mean(scaled * unit_rows, axis=-1, keepdims=True)
    )
    return (grad_in, jnp.sum(grad_norm * unit_rows, axis=0))


def swap(block, bit):
    pairs = [(i, i ^ bit) for i in range(lax.axis_size("tensor"))]
    return lax.ppermute(block, "tensor", pairs)


def gather_blocks(local_rows):
    if lax.axis_size("tensor") != NG:
        whole = lax.all_gather(local_rows, "tensor", axis=0, tiled=True)
        return jnp.split(whole, NG, axis=0)
    half = local_rows.shape[0] // 2
    one = swap(local_rows, 1)
    two = swap(local_rows, 2)
    top = swap(two[:half], 1)
    low = swap(one[half:], 2)
    return [local_rows, one, two, jnp.concatenate([top, low], axis=0)]


def scatter_blocks(make_block):
    if lax.axis_size("tensor") != NG:
        whole = jnp.concatenate([make_block(k) for k in range(NG)], axis=0)
        return lax.psum_scatter(
            whole.astype(jnp.bfloat16), "tensor", scatter_dimension=0, tiled=True
        ).astype(jnp.float32)
    three = make_block(3).astype(jnp.bfloat16)
    half = three.shape[0] // 2
    top = swap(three[:half], 1)
    low = swap(three[half:], 2)
    one = make_block(1)
    one = jnp.concatenate([one[:half], one[half:] + low.astype(jnp.float32)], axis=0)
    one = swap(one.astype(jnp.bfloat16), 1)
    two = make_block(2)
    two = jnp.concatenate([two[:half] + top.astype(jnp.float32), two[half:]], axis=0)
    two = swap(two.astype(jnp.bfloat16), 2)
    return make_block(0) + one.astype(jnp.float32) + two.astype(jnp.float32)


def gather_dp(piece):
    return lax.all_gather(piece, "dp", axis=0, tiled=True)


def scatter_dp(whole):
    return lax.psum_scatter(
        whole.astype(jnp.bfloat16), "dp", scatter_dimension=0, tiled=True
    ).astype(jnp.float32)


def score_block(single_query, every_key, key_mask):
    score_matrix = (
        jnp.einsum("wclz,icz->clwi", single_query, every_key, preferred_element_type=jnp.float32)
        * ATTN_SCALE
    )
    return jnp.where(key_mask[None, None], score_matrix, NEG_FILL)


FF_PARTS = 2


def local(
    tokens,
    cotangent,
    prompt_len,
    cont_len,
    w_query,
    key_weight,
    value_weight,
    w_out,
    w_gate,
    w_up,
    w_down,
    attn_gain,
    ffn_gain,
):
    portion = PROMPT_DEV
    group_rows = PROMPT_DEV + CONT
    dp_size = lax.axis_size("dp")
    prompt_rows = PROMPT_DEV * dp_size
    dp_index = lax.axis_index("dp")
    tensor_index = lax.axis_index("tensor")
    relative = lax.axis_size("tensor") == NG
    local_rows = tokens.shape[0]
    q_cols = w_query.shape[1]
    kv_cols = key_weight.shape[1]
    head_count = q_cols // HEAD_SIZE
    group_count = kv_cols // HEAD_SIZE
    repeat = head_count // group_count
    qkv_cols = q_cols + 2 * kv_cols
    ff_cols = w_gate.shape[1]
    part = ff_cols // FF_PARTS

    attn_pack = gather_dp(
        jnp.concatenate([w_query, key_weight, value_weight, w_out.T], axis=1)
    )
    full_qkv = attn_pack[:, :qkv_cols]
    full_out_t = attn_pack[:, qkv_cols:]
    down_t = w_down.T
    gate_parts, up_parts, down_parts = [], [], []
    for c in range(FF_PARTS):
        cols = slice(c * part, (c + 1) * part)
        gate_parts.append(gather_dp(w_gate[:, cols]))
        up_parts.append(gather_dp(w_up[:, cols]))
        down_parts.append(gather_dp(down_t[:, cols]))
    gains = gather_dp(jnp.stack([attn_gain, ffn_gain], axis=1)).astype(jnp.float32)
    gain_one = gains[:, 0]
    gain_two = gains[:, 1]

    order = [tensor_index ^ k if relative else k for k in range(NG)]
    lengths = jnp.stack([prompt_len[g] for g in order]) if relative else prompt_len
    col_ids = jnp.arange(group_rows)[None, :]
    starts = lengths[:, None]
    positions = jnp.where(
        col_ids < portion, dp_index * portion + col_ids, starts + col_ids - portion
    ).reshape(-1)
    valid_rows = jnp.where(
        col_ids < portion,
        dp_index * portion + col_ids < prompt_len[:, None],
        col_ids - portion < cont_len,
    ).reshape(-1)
    valid_local = lax.dynamic_slice_in_dim(
        valid_rows.astype(jnp.float32), tensor_index * local_rows, local_rows
    )
    cosine_table, sine_values = rope_tables(positions, HEAD_SIZE)

    resid_in = tokens.astype(jnp.float32)
    unit_one, scale_one = norm_parts(resid_in)
    normed_blocks = gather_blocks((unit_one * gain_one).astype(jnp.bfloat16))
    grad_y = cotangent.astype(jnp.float32) * valid_local[:, None]
    grad_ffn_blocks = gather_blocks((RESID_SCALE * grad_y).astype(jnp.bfloat16))

    normed = jnp.concatenate(normed_blocks, axis=0)
    qkv = project(normed, full_qkv)
    query_rot = apply_rotary(
        qkv[:, :q_cols].reshape(-1, head_count, HEAD_SIZE), cosine_table, sine_values
    ).astype(jnp.bfloat16)
    key_rot = apply_rotary(
        qkv[:, q_cols : q_cols + kv_cols].reshape(-1, group_count, HEAD_SIZE),
        cosine_table,
        sine_values,
    ).astype(jnp.bfloat16)
    query_grp = query_rot.reshape(NG, group_rows, group_count, repeat, HEAD_SIZE)
    kv_grp = jnp.concatenate(
        [key_rot.reshape(-1, kv_cols), qkv[:, q_cols + kv_cols :].astype(jnp.bfloat16)], axis=1
    ).reshape(NG, group_rows, 2 * kv_cols)
    prompt_kv = lax.all_gather(kv_grp[:, :portion], "dp", axis=0)

    def group_setup(k):
        key_mask = build_mask(dp_index * portion, lengths[k], portion, CONT, prompt_rows)
        kv_all = jnp.concatenate(
            [prompt_kv[:, k].reshape(prompt_rows, 2 * kv_cols), kv_grp[k, portion:]], axis=0
        )
        every_key = kv_all[:, :kv_cols].reshape(-1, group_count, HEAD_SIZE)
        every_value = kv_all[:, kv_cols:].reshape(-1, group_count, HEAD_SIZE)
        return key_mask, every_key, every_value

    kept = {}

    def forward_group(k):
        key_mask, every_key, every_value = group_setup(k)
        score_matrix = score_block(query_grp[k], every_key, key_mask)
        row_top = jnp.max(score_matrix, axis=-1, keepdims=True)
        weights = jnp.exp(score_matrix - row_top)
        row_total = jnp.sum(weights, axis=-1, keepdims=True)
        probability = (weights / row_total).astype(jnp.bfloat16)
        mixed = jnp.einsum(
            "yxks,syt->kyxt", probability, every_value, preferred_element_type=jnp.float32
        )
        mixed = mixed.reshape(group_rows, q_cols).astype(jnp.bfloat16)
        kept[k] = (row_top, row_total, mixed)
        return dot_back(mixed, full_out_t)

    hidden = resid_in + RESID_SCALE * scatter_blocks(forward_group)
    unit_two, scale_two = norm_parts(hidden)
    normed_two = jnp.concatenate(
        gather_blocks((unit_two * gain_two).astype(jnp.bfloat16)), axis=0
    )
    grad_ffn = jnp.concatenate(grad_ffn_blocks, axis=0)

    products, grad_gates, grad_ups = [], [], []
    gate_grads, up_grads, down_grads = [], [], []
    for c in range(FF_PARTS):
        gate_val = project(normed_two, gate_parts[c])
        up_val = project(normed_two, up_parts[c])
        sigmoid_gate = jax.nn.sigmoid(gate_val)
        product = (gate_val * sigmoid_gate * up_val).astype(jnp.bfloat16)
        down_grads.append(scatter_dp(dot_rows(grad_ffn, product)))
        grad_prod = project(grad_ffn, down_parts[c])
        grad_gate_val = (
            grad_prod * up_val * sigmoid_gate * (1.0 + gate_val * (1.0 - sigmoid_gate))
        ).astype(jnp.bfloat16)
        grad_up_val = (grad_prod * gate_val * sigmoid_gate).astype(jnp.bfloat16)
        gate_grads.append(scatter_dp(dot_rows(normed_two, grad_gate_val)))
        up_grads.append(scatter_dp(dot_rows(normed_two, grad_up_val)))
        products.append(product)
        grad_gates.append(grad_gate_val)
        grad_ups.append(grad_up_val)

    def rows_of(array, k):
        return array[k * group_rows : (k + 1) * group_rows]

    def ffn_back_block(k):
        total = 0.0
        for c in range(FF_PARTS):
            total = total + dot_back(rows_of(grad_gates[c], k), gate_parts[c])
            total = total + dot_back(rows_of(grad_ups[c], k), up_parts[c])
        return total

    def ffn_out_block(k):
        total = 0.0
        for c in range(FF_PARTS):
            total = total + dot_back(rows_of(products[c], k), down_parts[c])
        return total

    grad_normed_two = scatter_blocks(ffn_back_block)
    output = (hidden + RESID_SCALE * scatter_blocks(ffn_out_block)).astype(jnp.bfloat16)
    grad_hidden_norm, gain_two_part = norm_back(grad_normed_two, unit_two, scale_two, gain_two)
    grad_hidden = grad_y + grad_hidden_norm

    grad_attn_blocks = gather_blocks((RESID_SCALE * grad_hidden).astype(jnp.bfloat16))
    grad_attn = jnp.concatenate(grad_attn_blocks, axis=0)
    mixed_rows = jnp.concatenate([kept[k][2] for k in range(NG)], axis=0)
    grad_out = scatter_dp(dot_rows(grad_attn, mixed_rows)).T

    def backward_group(k):
        key_mask, every_key, every_value = group_setup(k)
        row_top, row_total, _ = kept[k]
        single_query = query_grp[k]
        single_gradient = (
            project(grad_attn_blocks[k], full_out_t)
            .astype(jnp.bfloat16)
            .reshape(group_rows, group_count, repeat, HEAD_SIZE)
        )
        score_matrix = score_block(single_query, every_key, key_mask)
        probability_rows = jnp.exp(score_matrix - row_top) / row_total
        grad_probs = jnp.einsum(
            "wclz,icz->clwi", single_gradient, every_value, preferred_element_type=jnp.float32
        )
        row_inner = jnp.sum(probability_rows * grad_probs, axis=-1, keepdims=True)
        score_gradient = (probability_rows * (grad_probs - row_inner)).astype(jnp.bfloat16)
        grad_query_one = (
            jnp.einsum(
                "yxks,syt->kyxt", score_gradient, every_key, preferred_element_type=jnp.float32
            )
            * ATTN_SCALE
        )
        grad_key_one = (
            jnp.einsum(
                "kjsv,skjb->vkb", score_gradient, single_query, preferred_element_type=jnp.float32
            )
            * ATTN_SCALE
        )
        grad_value_one = jnp.einsum(
            "kjsv,skjb->vkb",
            probability_rows.astype(jnp.bfloat16),
            single_gradient,
            preferred_element_type=jnp.float32,
        )
        grad_kv = jnp.concatenate(
            [grad_key_one.reshape(-1, kv_cols), grad_value_one.reshape(-1, kv_cols)], axis=1
        )
        return grad_query_one, grad_kv

    backs = [backward_group(k) for k in range(NG)]
    prompt_grad = jnp.stack(
        [b[1][:prompt_rows].reshape(dp_size, portion, 2 * kv_cols) for b in backs], axis=1
    ).reshape(dp_size * NG * portion, 2 * kv_cols)
    prompt_grad = scatter_dp(prompt_grad).reshape(NG, portion, 2 * kv_cols)
    kv_grad = jnp.concatenate(
        [prompt_grad, jnp.stack([b[1][prompt_rows:] for b in backs])], axis=1
    ).reshape(NG * group_rows, 2 * kv_cols)
    query_grad = unrotate(
        jnp.stack([b[0] for b in backs]).reshape(-1, head_count, HEAD_SIZE),
        cosine_table,
        sine_values,
    ).reshape(-1, q_cols)
    key_grad = unrotate(
        kv_grad[:, :kv_cols].reshape(-1, group_count, HEAD_SIZE), cosine_table, sine_values
    ).reshape(-1, kv_cols)
    qkv_grad = jnp.concatenate([query_grad, key_grad, kv_grad[:, kv_cols:]], axis=1).astype(
        jnp.bfloat16
    )
    grad_normed = scatter_blocks(lambda k: dot_back(rows_of(qkv_grad, k), full_qkv))
    qkv_w_grad = scatter_dp(dot_rows(normed, qkv_grad))
    grad_input_norm, gain_one_part = norm_back(grad_normed, unit_one, scale_one, gain_one)
    input_grad = grad_hidden + grad_input_norm
    gain_grads = lax.psum_scatter(
        jnp.stack([gain_one_part, gain_two_part], axis=1),
        ("dp", "tensor"),
        scatter_dimension=0,
        tiled=True,
    )
    return (
        output,
        input_grad,
        qkv_w_grad[:, :q_cols],
        qkv_w_grad[:, q_cols : q_cols + kv_cols],
        qkv_w_grad[:, q_cols + kv_cols :],
        grad_out,
        jnp.concatenate(gate_grads, axis=1),
        jnp.concatenate(up_grads, axis=1),
        jnp.concatenate(down_grads, axis=1).T,
        gain_grads[:, 0],
        gain_grads[:, 1],
    )


def solution(mesh):
    placed = (
        P(("dp", "tensor"), None),
        P(("dp", "tensor"), None),
        P(),
        P(None, "dp"),
        P("dp", "tensor"),
        P("dp", "tensor"),
        P("dp", "tensor"),
        P("tensor", "dp"),
        P("dp", "tensor"),
        P("dp", "tensor"),
        P("tensor", "dp"),
        P("dp"),
        P("dp"),
    )
    return jax.shard_map(
        local,
        mesh=mesh,
        in_specs=placed,
        out_specs=(
            P(("dp", "tensor"), None),
            P(("dp", "tensor"), None),
            P("dp", "tensor"),
            P("dp", "tensor"),
            P("dp", "tensor"),
            P("tensor", "dp"),
            P("dp", "tensor"),
            P("dp", "tensor"),
            P("tensor", "dp"),
            P(("dp", "tensor")),
            P(("dp", "tensor")),
        ),
        check_vma=False,
    )
```

```python
import jax
import jax.numpy as jnp
from jax import lax
from jax.sharding import PartitionSpec as P

HEAD_SIZE = 64
NG = 4
PROMPT_DEV = 128
CONT = 256


EPS = 1e-05
THETA = 10000000.0
ATTN_SCALE = 0.015625
RESID_SCALE = 0.22
NEG_FILL = -1e30


def project(left_mat, right_mat):
    return jnp.dot(left_mat, right_mat, preferred_element_type=jnp.float32)


def dot_rows(left_mat, right_mat):
    return lax.dot_general(
        left_mat, right_mat, (((0,), (0,)), ((), ())), preferred_element_type=jnp.float32
    )


def dot_back(left_mat, right_mat):
    return lax.dot_general(
        left_mat, right_mat, (((1,), (1,)), ((), ())), preferred_element_type=jnp.float32
    )


def rope_tables(positions, head_width):
    half_width = head_width // 2
    frequency = THETA ** (-(jnp.arange(half_width).astype(jnp.float32) * 2.0) / head_width)
    angles = positions.astype(jnp.float32)[:, None] * frequency[None, :]
    angles = jnp.concatenate([angles, angles], axis=1)
    return (jnp.cos(angles), jnp.sin(angles))


def apply_rotary(values, cosine_table, sine_values):
    half_width = values.shape[-1] // 2
    turned = jnp.concatenate([-values[..., half_width:], values[..., :half_width]], axis=-1)
    return values * cosine_table[:, None, :] + turned * sine_values[:, None, :]


def unrotate(values, cosine_table, sine_values):
    half_width = values.shape[-1] // 2
    scaled_sin = values * sine_values[:, None, :]
    turned = jnp.concatenate([scaled_sin[..., half_width:], -scaled_sin[..., :half_width]], axis=-1)
    return values * cosine_table[:, None, :] + turned


def build_mask(base_row, prompt_length, portion_rows, cont_rows, prompt_row_count):
    row_ids = jnp.arange(portion_rows + cont_rows)[:, None]
    key_ids = jnp.arange(prompt_row_count + cont_rows)[None, :]
    in_prompt = key_ids < prompt_row_count
    prompt_part = in_prompt & (key_ids <= base_row + row_ids)
    cont_part = jnp.where(
        in_prompt, key_ids < prompt_length, key_ids - prompt_row_count <= row_ids - portion_rows
    )
    return jnp.where(row_ids < portion_rows, prompt_part, cont_part)


def norm_parts(values):
    row_scale = lax.rsqrt(jnp.mean(values * values, axis=-1, keepdims=True) + EPS)
    return (values * row_scale, row_scale)


def norm_back(grad_norm, unit_rows, row_scale, gain_vec):
    scaled = grad_norm * gain_vec
    grad_in = row_scale * (
        scaled - unit_rows * jnp.mean(scaled * unit_rows, axis=-1, keepdims=True)
    )
    return (grad_in, jnp.sum(grad_norm * unit_rows, axis=0))


def swap(block, bit):
    pairs = [(i, i ^ bit) for i in range(lax.axis_size("tensor"))]
    return lax.ppermute(block, "tensor", pairs)


def gather_blocks(local_rows):
    if lax.axis_size("tensor") != NG:
        whole = lax.all_gather(local_rows, "tensor", axis=0, tiled=True)
        return jnp.split(whole, NG, axis=0)
    half = local_rows.shape[0] // 2
    one = swap(local_rows, 1)
    two = swap(local_rows, 2)
    top = swap(two[:half], 1)
    low = swap(one[half:], 2)
    return [local_rows, one, two, jnp.concatenate([top, low], axis=0)]


def scatter_blocks(make_block):
    if lax.axis_size("tensor") != NG:
        whole = jnp.concatenate([make_block(k) for k in range(NG)], axis=0)
        return lax.psum_scatter(
            whole.astype(jnp.bfloat16), "tensor", scatter_dimension=0, tiled=True
        ).astype(jnp.float32)
    three = make_block(3).astype(jnp.bfloat16)
    half = three.shape[0] // 2
    top = swap(three[:half], 1)
    low = swap(three[half:], 2)
    one = make_block(1)
    one = jnp.concatenate([one[:half], one[half:] + low.astype(jnp.float32)], axis=0)
    one = swap(one.astype(jnp.bfloat16), 1)
    two = make_block(2)
    two = jnp.concatenate([two[:half] + top.astype(jnp.float32), two[half:]], axis=0)
    two = swap(two.astype(jnp.bfloat16), 2)
    return make_block(0) + one.astype(jnp.float32) + two.astype(jnp.float32)


def tie(value, first):
    return lax.optimization_barrier((value, first))[0]


def gather_dp(piece):
    return lax.all_gather(piece, "dp", axis=0, tiled=True)


def scatter_dp(whole):
    return lax.psum_scatter(
        whole.astype(jnp.bfloat16), "dp", scatter_dimension=0, tiled=True
    ).astype(jnp.float32)


def score_block(single_query, every_key, key_mask):
    score_matrix = (
        jnp.einsum("wclz,icz->clwi", single_query, every_key, preferred_element_type=jnp.float32)
        * ATTN_SCALE
    )
    return jnp.where(key_mask[None, None], score_matrix, NEG_FILL)


FF_PARTS = 1


def local(
    tokens,
    cotangent,
    prompt_len,
    cont_len,
    w_query,
    key_weight,
    value_weight,
    w_out,
    w_gate,
    w_up,
    w_down,
    attn_gain,
    ffn_gain,
):
    portion = PROMPT_DEV
    group_rows = PROMPT_DEV + CONT
    dp_size = lax.axis_size("dp")
    prompt_rows = PROMPT_DEV * dp_size
    dp_index = lax.axis_index("dp")
    tensor_index = lax.axis_index("tensor")
    relative = lax.axis_size("tensor") == NG
    local_rows = tokens.shape[0]
    q_cols = w_query.shape[1]
    kv_cols = key_weight.shape[1]
    head_count = q_cols // HEAD_SIZE
    group_count = kv_cols // HEAD_SIZE
    repeat = head_count // group_count
    qkv_cols = q_cols + 2 * kv_cols
    ff_cols = w_gate.shape[1]
    part = ff_cols // FF_PARTS

    attn_pack = gather_dp(
        jnp.concatenate([w_query, key_weight, value_weight, w_out.T], axis=1)
    )
    full_qkv = attn_pack[:, :qkv_cols]
    full_out_t = attn_pack[:, qkv_cols:]
    down_t = w_down.T
    gate_parts, up_parts, down_parts = [], [], []
    for c in range(FF_PARTS):
        cols = slice(c * part, (c + 1) * part)
        gate_parts.append(gather_dp(w_gate[:, cols]))
        up_parts.append(gather_dp(w_up[:, cols]))
        down_parts.append(gather_dp(down_t[:, cols]))
    gains = gather_dp(jnp.stack([attn_gain, ffn_gain], axis=1)).astype(jnp.float32)
    gain_one = gains[:, 0]
    gain_two = gains[:, 1]

    order = [tensor_index ^ k if relative else k for k in range(NG)]
    lengths = jnp.stack([prompt_len[g] for g in order]) if relative else prompt_len
    col_ids = jnp.arange(group_rows)[None, :]
    starts = lengths[:, None]
    positions = jnp.where(
        col_ids < portion, dp_index * portion + col_ids, starts + col_ids - portion
    ).reshape(-1)
    valid_rows = jnp.where(
        col_ids < portion,
        dp_index * portion + col_ids < prompt_len[:, None],
        col_ids - portion < cont_len,
    ).reshape(-1)
    valid_local = lax.dynamic_slice_in_dim(
        valid_rows.astype(jnp.float32), tensor_index * local_rows, local_rows
    )
    cosine_table, sine_values = rope_tables(positions, HEAD_SIZE)

    resid_in = tokens.astype(jnp.float32)
    unit_one, scale_one = norm_parts(resid_in)
    token_rows = jnp.concatenate(gather_blocks(tokens), axis=0).astype(jnp.float32)
    grad_y = cotangent.astype(jnp.float32) * valid_local[:, None]
    grad_ffn_blocks = gather_blocks((RESID_SCALE * grad_y).astype(jnp.bfloat16))

    normed = (norm_parts(token_rows)[0] * gain_one).astype(jnp.bfloat16)
    qkv = project(normed, full_qkv)
    query_rot = apply_rotary(
        qkv[:, :q_cols].reshape(-1, head_count, HEAD_SIZE), cosine_table, sine_values
    ).astype(jnp.bfloat16)
    key_rot = apply_rotary(
        qkv[:, q_cols : q_cols + kv_cols].reshape(-1, group_count, HEAD_SIZE),
        cosine_table,
        sine_values,
    ).astype(jnp.bfloat16)
    query_grp = query_rot.reshape(NG, group_rows, group_count, repeat, HEAD_SIZE)
    kv_grp = jnp.concatenate(
        [key_rot.reshape(-1, kv_cols), qkv[:, q_cols + kv_cols :].astype(jnp.bfloat16)], axis=1
    ).reshape(NG, group_rows, 2 * kv_cols)
    prompt_kv = lax.all_gather(kv_grp[:, :portion], "dp", axis=0)

    def group_setup(k):
        key_mask = build_mask(dp_index * portion, lengths[k], portion, CONT, prompt_rows)
        kv_all = jnp.concatenate(
            [prompt_kv[:, k].reshape(prompt_rows, 2 * kv_cols), kv_grp[k, portion:]], axis=0
        )
        every_key = kv_all[:, :kv_cols].reshape(-1, group_count, HEAD_SIZE)
        every_value = kv_all[:, kv_cols:].reshape(-1, group_count, HEAD_SIZE)
        return key_mask, every_key, every_value

    kept = {}

    def forward_group(k):
        key_mask, every_key, every_value = group_setup(k)
        score_matrix = score_block(query_grp[k], every_key, key_mask)
        row_top = jnp.max(score_matrix, axis=-1, keepdims=True)
        weights = jnp.exp(score_matrix - row_top)
        row_total = jnp.sum(weights, axis=-1, keepdims=True)
        probability = (weights / row_total).astype(jnp.bfloat16)
        mixed = jnp.einsum(
            "yxks,syt->kyxt", probability, every_value, preferred_element_type=jnp.float32
        )
        mixed = mixed.reshape(group_rows, q_cols).astype(jnp.bfloat16)
        kept[k] = (row_top, row_total, mixed)
        return dot_back(mixed, full_out_t)

    hidden = resid_in + RESID_SCALE * scatter_blocks(forward_group)
    unit_two, scale_two = norm_parts(hidden)
    normed_two = jnp.concatenate(
        gather_blocks((unit_two * gain_two).astype(jnp.bfloat16)), axis=0
    )
    grad_ffn = jnp.concatenate(grad_ffn_blocks, axis=0)

    products, grad_gates, grad_ups = [], [], []
    gate_grads, up_grads, down_grads = [], [], []
    for c in range(FF_PARTS):
        gate_val = project(normed_two, gate_parts[c])
        up_val = project(normed_two, up_parts[c])
        sigmoid_gate = jax.nn.sigmoid(gate_val)
        product = (gate_val * sigmoid_gate * up_val).astype(jnp.bfloat16)
        down_sum = dot_rows(grad_ffn, product).astype(jnp.bfloat16)
        down_grads.append(scatter_dp(down_sum))
        grad_prod = project(tie(grad_ffn, down_sum), down_parts[c])
        grad_gate_val = (
            grad_prod * up_val * sigmoid_gate * (1.0 + gate_val * (1.0 - sigmoid_gate))
        ).astype(jnp.bfloat16)
        grad_up_val = (grad_prod * gate_val * sigmoid_gate).astype(jnp.bfloat16)
        gate_sum = dot_rows(normed_two, grad_gate_val).astype(jnp.bfloat16)
        gate_grads.append(scatter_dp(gate_sum))
        up_sum = dot_rows(normed_two, grad_up_val).astype(jnp.bfloat16)
        up_grads.append(scatter_dp(up_sum))
        grad_gate_val, grad_up_val = tie((grad_gate_val, grad_up_val), gate_sum)
        products.append(product)
        grad_gates.append(grad_gate_val)
        grad_ups.append(grad_up_val)

    def rows_of(array, k):
        return array[k * group_rows : (k + 1) * group_rows]

    def ffn_back_block(k):
        total = 0.0
        for c in range(FF_PARTS):
            total = total + dot_back(rows_of(grad_gates[c], k), gate_parts[c])
            total = total + dot_back(rows_of(grad_ups[c], k), up_parts[c])
        return total

    def ffn_out_block(k):
        total = 0.0
        for c in range(FF_PARTS):
            total = total + dot_back(rows_of(products[c], k), down_parts[c])
        return total

    grad_normed_two = scatter_blocks(ffn_back_block)
    output = (hidden + RESID_SCALE * scatter_blocks(ffn_out_block)).astype(jnp.bfloat16)
    grad_hidden_norm, gain_two_part = norm_back(grad_normed_two, unit_two, scale_two, gain_two)
    grad_hidden = grad_y + grad_hidden_norm

    grad_attn_blocks = gather_blocks((RESID_SCALE * grad_hidden).astype(jnp.bfloat16))
    grad_attn = jnp.concatenate(grad_attn_blocks, axis=0)
    mixed_rows = jnp.concatenate([kept[k][2] for k in range(NG)], axis=0)
    out_sum = dot_rows(grad_attn, mixed_rows).astype(jnp.bfloat16)
    grad_out = scatter_dp(out_sum).T
    grad_attn_blocks[1:] = tie(grad_attn_blocks[1:], up_sum)
    grad_attn_blocks[1], down_grads = lax.optimization_barrier((grad_attn_blocks[1], down_grads))
    grad_attn_blocks[3], gate_grads = lax.optimization_barrier((grad_attn_blocks[3], gate_grads))

    def backward_group(k):
        key_mask, every_key, every_value = group_setup(k)
        row_top, row_total, _ = kept[k]
        single_query = query_grp[k]
        single_gradient = (
            project(grad_attn_blocks[k], full_out_t)
            .astype(jnp.bfloat16)
            .reshape(group_rows, group_count, repeat, HEAD_SIZE)
        )
        score_matrix = score_block(single_query, every_key, key_mask)
        probability_rows = jnp.exp(score_matrix - row_top) / row_total
        grad_probs = jnp.einsum(
            "wclz,icz->clwi", single_gradient, every_value, preferred_element_type=jnp.float32
        )
        row_inner = jnp.sum(probability_rows * grad_probs, axis=-1, keepdims=True)
        score_gradient = (probability_rows * (grad_probs - row_inner)).astype(jnp.bfloat16)
        grad_query_one = (
            jnp.einsum(
                "yxks,syt->kyxt", score_gradient, every_key, preferred_element_type=jnp.float32
            )
            * ATTN_SCALE
        )
        grad_key_one = (
            jnp.einsum(
                "kjsv,skjb->vkb", score_gradient, single_query, preferred_element_type=jnp.float32
            )
            * ATTN_SCALE
        )
        grad_value_one = jnp.einsum(
            "kjsv,skjb->vkb",
            probability_rows.astype(jnp.bfloat16),
            single_gradient,
            preferred_element_type=jnp.float32,
        )
        grad_kv = jnp.concatenate(
            [grad_key_one.reshape(-1, kv_cols), grad_value_one.reshape(-1, kv_cols)], axis=1
        )
        return grad_query_one, grad_kv

    backs = [backward_group(k) for k in range(NG)]
    prompt_grad = jnp.stack(
        [b[1][:prompt_rows].reshape(dp_size, portion, 2 * kv_cols) for b in backs], axis=1
    ).reshape(dp_size * NG * portion, 2 * kv_cols)
    prompt_grad, up_grads = lax.optimization_barrier((prompt_grad, up_grads))
    prompt_grad = scatter_dp(prompt_grad).reshape(NG, portion, 2 * kv_cols)
    kv_grad = jnp.concatenate(
        [prompt_grad, jnp.stack([b[1][prompt_rows:] for b in backs])], axis=1
    ).reshape(NG * group_rows, 2 * kv_cols)
    query_grad = unrotate(
        jnp.stack([b[0] for b in backs]).reshape(-1, head_count, HEAD_SIZE),
        cosine_table,
        sine_values,
    ).reshape(-1, q_cols)
    key_grad = unrotate(
        kv_grad[:, :kv_cols].reshape(-1, group_count, HEAD_SIZE), cosine_table, sine_values
    ).reshape(-1, kv_cols)
    qkv_grad = jnp.concatenate([query_grad, key_grad, kv_grad[:, kv_cols:]], axis=1).astype(
        jnp.bfloat16
    )
    grad_normed = scatter_blocks(lambda k: dot_back(rows_of(qkv_grad, k), full_qkv))
    qkv_w_grad = scatter_dp(dot_rows(normed, qkv_grad))
    grad_input_norm, gain_one_part = norm_back(grad_normed, unit_one, scale_one, gain_one)
    input_grad = grad_hidden + grad_input_norm
    gain_sums = lax.psum(jnp.stack([gain_one_part, gain_two_part]), ("dp", "tensor"))
    gain_cols = gain_sums.shape[1] // (dp_size * lax.axis_size("tensor"))
    gain_start = (dp_index * lax.axis_size("tensor") + tensor_index) * gain_cols
    gain_grads = lax.dynamic_slice_in_dim(gain_sums, gain_start, gain_cols, axis=1)
    return (
        output,
        input_grad,
        qkv_w_grad[:, :q_cols],
        qkv_w_grad[:, q_cols : q_cols + kv_cols],
        qkv_w_grad[:, q_cols + kv_cols :],
        grad_out,
        jnp.concatenate(gate_grads, axis=1),
        jnp.concatenate(up_grads, axis=1),
        jnp.concatenate(down_grads, axis=1).T,
        gain_grads[0],
        gain_grads[1],
    )


def solution(mesh):
    placed = (
        P(("dp", "tensor"), None),
        P(("dp", "tensor"), None),
        P(),
        P(None, "dp"),
        P("dp", "tensor"),
        P("dp", "tensor"),
        P("dp", "tensor"),
        P("tensor", "dp"),
        P("dp", "tensor"),
        P("dp", "tensor"),
        P("tensor", "dp"),
        P("dp"),
        P("dp"),
    )
    return jax.shard_map(
        local,
        mesh=mesh,
        in_specs=placed,
        out_specs=(
            P(("dp", "tensor"), None),
            P(("dp", "tensor"), None),
            P("dp", "tensor"),
            P("dp", "tensor"),
            P("dp", "tensor"),
            P("tensor", "dp"),
            P("dp", "tensor"),
            P("dp", "tensor"),
            P("tensor", "dp"),
            P(("dp", "tensor")),
            P(("dp", "tensor")),
        ),
        check_vma=False,
    )
```

```python
import functools

import jax
import jax.numpy as jnp
from jax import lax
from jax.experimental import pallas as pl
from jax.experimental.pallas import tpu as pltpu
from jax.sharding import PartitionSpec as P

HEAD_SIZE = 64
NG = 4
PROMPT_DEV = 128
CONT = 256


EPS = 1e-05
THETA = 10000000.0
ATTN_SCALE = 0.015625
RESID_SCALE = 0.22
NEG_FILL = -1e30


def project(left_mat, right_mat):
    return jnp.dot(left_mat, right_mat, preferred_element_type=jnp.float32)


def dot_rows(left_mat, right_mat):
    return lax.dot_general(
        left_mat, right_mat, (((0,), (0,)), ((), ())), preferred_element_type=jnp.float32
    )


def dot_back(left_mat, right_mat):
    return lax.dot_general(
        left_mat, right_mat, (((1,), (1,)), ((), ())), preferred_element_type=jnp.float32
    )


def rope_tables(positions, head_width):
    half_width = head_width // 2
    frequency = THETA ** (-(jnp.arange(half_width).astype(jnp.float32) * 2.0) / head_width)
    angles = positions.astype(jnp.float32)[:, None] * frequency[None, :]
    angles = jnp.concatenate([angles, angles], axis=1)
    return (jnp.cos(angles), jnp.sin(angles))


def norm_parts(values):
    row_scale = lax.rsqrt(jnp.mean(values * values, axis=-1, keepdims=True) + EPS)
    return (values * row_scale, row_scale)


def norm_back(grad_norm, unit_rows, row_scale, gain_vec):
    scaled = grad_norm * gain_vec
    grad_in = row_scale * (
        scaled - unit_rows * jnp.mean(scaled * unit_rows, axis=-1, keepdims=True)
    )
    return (grad_in, jnp.sum(grad_norm * unit_rows, axis=0))


def swap(block, bit):
    pairs = [(i, i ^ bit) for i in range(lax.axis_size("tensor"))]
    return lax.ppermute(block, "tensor", pairs)


def gather_blocks(local_rows):
    if lax.axis_size("tensor") != NG:
        whole = lax.all_gather(local_rows, "tensor", axis=0, tiled=True)
        return jnp.split(whole, NG, axis=0)
    half = local_rows.shape[0] // 2
    one = swap(local_rows, 1)
    two = swap(local_rows, 2)
    top = swap(two[:half], 1)
    low = swap(one[half:], 2)
    return [local_rows, one, two, jnp.concatenate([top, low], axis=0)]


def scatter_blocks(make_block):
    if lax.axis_size("tensor") != NG:
        whole = jnp.concatenate([make_block(k) for k in range(NG)], axis=0)
        return lax.psum_scatter(
            whole.astype(jnp.bfloat16), "tensor", scatter_dimension=0, tiled=True
        ).astype(jnp.float32)
    three = make_block(3).astype(jnp.bfloat16)
    half = three.shape[0] // 2
    top = swap(three[:half], 1)
    low = swap(three[half:], 2)
    one = make_block(1)
    one = jnp.concatenate([one[:half], one[half:] + low.astype(jnp.float32)], axis=0)
    one = swap(one.astype(jnp.bfloat16), 1)
    two = make_block(2)
    two = jnp.concatenate([two[:half] + top.astype(jnp.float32), two[half:]], axis=0)
    two = swap(two.astype(jnp.bfloat16), 2)
    return make_block(0) + one.astype(jnp.float32) + two.astype(jnp.float32)


def tie(value, first):
    return lax.optimization_barrier((value, first))[0]


def gather_dp(piece):
    return lax.all_gather(piece, "dp", axis=0, tiled=True)


def scatter_dp(whole):
    return lax.psum_scatter(
        whole.astype(jnp.bfloat16), "dp", scatter_dimension=0, tiled=True
    ).astype(jnp.float32)


def swap_dp(block, bits):
    pairs = [(i, i ^ bits) for i in range(lax.axis_size("dp"))]
    return lax.ppermute(block, "dp", pairs)


def gather_prompt(block):
    if lax.axis_size("dp") != FAST_DP:
        return lax.all_gather(block, "dp", axis=0)
    mine = jnp.stack([block] + [swap_dp(block, bits) for bits in (2, 4, 6)])
    return jnp.stack([mine, swap_dp(mine, 1)], axis=1).reshape(FAST_DP, *block.shape)


def scatter_prompt(blocks):
    if lax.axis_size("dp") != FAST_DP:
        shape = blocks.shape[1:]
        return scatter_dp(blocks.reshape(-1, shape[-1])).reshape(shape)
    pairs = blocks.reshape(FAST_DP // 2, 2, *blocks.shape[1:])
    total = pairs[:, 0].astype(jnp.float32) + swap_dp(pairs[:, 1], 1).astype(jnp.float32)
    sent = total.astype(jnp.bfloat16)
    for r in (1, 2, 3):
        total = total.at[0].add(swap_dp(sent[r], 2 * r).astype(jnp.float32))
    return total[0]


def scatter_gain(part):
    for axis in ("dp", "tensor"):
        size = lax.axis_size(axis)
        index = lax.axis_index(axis)
        bit = size // 2
        while bit:
            halves = part.reshape(2, -1)
            side = (index // bit) % 2
            keep = jnp.where(side == 0, halves[0], halves[1])
            send = jnp.where(side == 0, halves[1], halves[0])
            part = keep + lax.ppermute(send, axis, [(i, i ^ bit) for i in range(size)])
            bit //= 2
    return part


FAST_DP = 8
LANES = 128
LOG2E = 1.4426950408889634
SCORE_MUL = ATTN_SCALE * LOG2E


def dot_nt(a, b):
    return lax.dot_general(a, b, (((1,), (1,)), ((), ())), preferred_element_type=jnp.float32)


def dot_tn(a, b):
    return lax.dot_general(a, b, (((0,), (0,)), ((), ())), preferred_element_type=jnp.float32)


def lane_of(shape):
    return lax.broadcasted_iota(jnp.int32, shape, len(shape) - 1)


def half_masks(block):
    low = (lane_of((1, LANES)) < HEAD_SIZE).astype(jnp.float32).astype(jnp.bfloat16)
    return block * low, block * (1 - low)


def key_limits(scalar_ref, group_rows, keys):
    row = lax.broadcasted_iota(jnp.int32, (group_rows, keys), 0)
    key = lax.broadcasted_iota(jnp.int32, (group_rows, keys), 1) ^ scalar_ref[2]
    limit = jnp.where(row < PROMPT_DEV, scalar_ref[0] + row + 1, scalar_ref[1])
    return key < limit


def own_allowed():
    row = lax.broadcasted_iota(jnp.int32, (CONT, CONT), 0)
    return lax.broadcasted_iota(jnp.int32, (CONT, CONT), 1) <= row


def attend_kernel(scalar_ref, q_ref, kp_ref, vp_ref, kc_ref, vc_ref, o_ref, stat_ref):
    pair = pl.program_id(0)
    rows = q_ref.shape[0]
    keys = kp_ref.shape[1] * kp_ref.shape[3]
    kp = kp_ref[...].reshape(keys, LANES)
    vp = vp_ref[...].reshape(keys, LANES)
    kc = kc_ref[...].reshape(CONT, LANES)
    vc = vc_ref[...].reshape(CONT, LANES)
    allowed = key_limits(scalar_ref, rows, keys)
    own = own_allowed()
    lane = lane_of((rows, LANES))

    @pl.when(pair == 0)
    def _():
        stat_ref[...] = jnp.zeros_like(stat_ref)

    outs = []
    for side, q in enumerate(half_masks(q_ref[...])):
        sp = jnp.where(allowed, dot_nt(q, kp) * SCORE_MUL, NEG_FILL)
        sc = jnp.where(own, dot_nt(q[PROMPT_DEV:], kc) * SCORE_MUL, NEG_FILL)
        top = jnp.max(sp, axis=1, keepdims=True)
        top_c = jnp.maximum(top[PROMPT_DEV:], jnp.max(sc, axis=1, keepdims=True))
        top = jnp.concatenate([top[:PROMPT_DEV], top_c], axis=0)
        ep = jnp.exp2(sp - top)
        ec = jnp.exp2(sc - top_c)
        total = jnp.sum(ep, axis=1, keepdims=True)
        total_c = total[PROMPT_DEV:] + jnp.sum(ec, axis=1, keepdims=True)
        total = jnp.concatenate([total[:PROMPT_DEV], total_c], axis=0)
        mixed = jnp.dot(ep.astype(jnp.bfloat16), vp, preferred_element_type=jnp.float32)
        mixed_c = jnp.dot(ec.astype(jnp.bfloat16), vc, preferred_element_type=jnp.float32)
        mixed = jnp.concatenate(
            [mixed[:PROMPT_DEV], mixed[PROMPT_DEV:] + mixed_c], axis=0
        )
        outs.append(mixed / total)
        stat = top + jnp.log2(total)
        stat_ref[...] = jnp.where(lane == 2 * pair + side, stat, stat_ref[...])
    o_ref[...] = jnp.where(lane < HEAD_SIZE, outs[0], outs[1]).astype(jnp.bfloat16)


def attend_back_kernel(
    scalar_ref, q_ref, g_ref, stat_ref, kp_ref, vp_ref, kc_ref, vc_ref, cos_ref, sin_ref,
    dq_ref, prompt_ref, own_ref, dkp_ref, dvp_ref, dkc_ref, dvc_ref, *, share, kv_heads
):
    pair = pl.program_id(0)
    rows = q_ref.shape[0]
    keys = kp_ref.shape[1] * kp_ref.shape[3]
    kp = kp_ref[...].reshape(keys, LANES)
    vp = vp_ref[...].reshape(keys, LANES)
    kc = kc_ref[...].reshape(CONT, LANES)
    vc = vc_ref[...].reshape(CONT, LANES)
    allowed = key_limits(scalar_ref, rows, keys)
    own = own_allowed()
    lane = lane_of((rows, LANES))

    @pl.when(pair % share == 0)
    def _():
        for ref in (dkp_ref, dvp_ref, dkc_ref, dvc_ref):
            ref[...] = jnp.zeros_like(ref)

    dqs = []
    sides = zip(half_masks(q_ref[...]), half_masks(g_ref[...]))
    for side, (q, g) in enumerate(sides):
        stat = jnp.sum(
            jnp.where(lane == 2 * pair + side, stat_ref[...], 0.0), axis=1, keepdims=True
        )
        pp = jnp.where(allowed, jnp.exp2(dot_nt(q, kp) * SCORE_MUL - stat), 0.0)
        pc = jnp.where(
            own, jnp.exp2(dot_nt(q[PROMPT_DEV:], kc) * SCORE_MUL - stat[PROMPT_DEV:]), 0.0
        )
        gp = dot_nt(g, vp)
        gc = dot_nt(g[PROMPT_DEV:], vc)
        inner = jnp.sum(pp * gp, axis=1, keepdims=True)
        inner_c = inner[PROMPT_DEV:] + jnp.sum(pc * gc, axis=1, keepdims=True)
        inner = jnp.concatenate([inner[:PROMPT_DEV], inner_c], axis=0)
        sp = (pp * (gp - inner)).astype(jnp.bfloat16)
        sc = (pc * (gc - inner_c)).astype(jnp.bfloat16)
        dq = jnp.dot(sp, kp, preferred_element_type=jnp.float32)
        dq_c = jnp.dot(sc, kc, preferred_element_type=jnp.float32)
        dqs.append(jnp.concatenate([dq[:PROMPT_DEV], dq[PROMPT_DEV:] + dq_c], axis=0))
        dkp_ref[...] += dot_tn(sp, q)
        dkc_ref[...] += dot_tn(sc, q[PROMPT_DEV:])
        dvp_ref[...] += dot_tn(pp.astype(jnp.bfloat16), g)
        dvc_ref[...] += dot_tn(pc.astype(jnp.bfloat16), g[PROMPT_DEV:])
    dq = jnp.where(lane < HEAD_SIZE, dqs[0], dqs[1]) * ATTN_SCALE
    dq_ref[...] = turn(dq, cos_ref[...], -sin_ref[...]).astype(jnp.bfloat16)

    for head in range(kv_heads):

        @pl.when(pair == (head + 1) * share - 1)
        def _(head=head):
            key_at = head * HEAD_SIZE
            value_at = (kv_heads + head) * HEAD_SIZE
            put_half(prompt_ref, dkp_ref[...] * ATTN_SCALE, key_at)
            put_half(prompt_ref, dvp_ref[...], value_at)
            put_half(own_ref, dkc_ref[...] * ATTN_SCALE, key_at)
            put_half(own_ref, dvc_ref[...], value_at)


def put_half(out_ref, total, at):
    total = total + pltpu.roll(total, HEAD_SIZE, 1)
    tile = pl.ds(at // LANES * LANES, LANES)
    mine = lane_of(total.shape) // HEAD_SIZE == at % LANES // HEAD_SIZE
    kept = out_ref[:, tile].astype(jnp.float32)
    out_ref[:, tile] = jnp.where(mine, total, kept).astype(out_ref.dtype)


def turn(u, cos, sin):
    lane = lane_of(u.shape) % HEAD_SIZE
    half = HEAD_SIZE // 2
    moved = jnp.where(lane < half, -pltpu.roll(u, LANES - half, 1), pltpu.roll(u, half, 1))
    return u * cos + moved * sin


def rope_kernel(u_ref, cos_ref, sin_ref, o_ref, *, turned):
    for start in range(0, u_ref.shape[1], LANES):
        u = u_ref[:, start : start + LANES]
        if start < turned:
            r = turn(u, cos_ref[...], sin_ref[...])
            if start + LANES > turned:
                r = jnp.where(lane_of(u.shape) < turned - start, r, u)
            u = r
        o_ref[:, start : start + LANES] = u.astype(jnp.bfloat16)


def rope(u, cos, sin, turned, block):
    n, cols = u.shape
    return pl.pallas_call(
        functools.partial(rope_kernel, turned=turned),
        grid=(n // block,),
        in_specs=[
            pl.BlockSpec((block, cols), lambda i: (i, 0)),
            pl.BlockSpec((block, LANES), lambda i: (i, 0)),
            pl.BlockSpec((block, LANES), lambda i: (i, 0)),
        ],
        out_specs=pl.BlockSpec((block, cols), lambda i: (i, 0)),
        out_shape=jax.ShapeDtypeStruct((n, cols), jnp.bfloat16),
        name="rope",
    )(u, cos, sin)


def key_specs(k, dp_size, portion, share):
    prompt = pl.BlockSpec(
        (1, dp_size, 1, portion, LANES), lambda p, s: (p // share, 0, k, 0, 0)
    )
    own = pl.BlockSpec((1, 1, CONT, LANES), lambda p, s: (p // share, k, 0, 0))
    return [prompt, prompt, own, own]


def attend(k, scalars, qkv, keys, q_cols, group_rows):
    dp_size, portion = keys[0].shape[1], keys[0].shape[3]
    kv_heads = keys[0].shape[0]
    pairs = q_cols // LANES
    share = pairs // kv_heads
    return pl.pallas_call(
        attend_kernel,
        grid_spec=pltpu.PrefetchScalarGridSpec(
            num_scalar_prefetch=1,
            grid=(pairs,),
            in_specs=[pl.BlockSpec((group_rows, LANES), lambda p, s: (k, p))]
            + key_specs(k, dp_size, portion, share),
            out_specs=[
                pl.BlockSpec((group_rows, LANES), lambda p, s: (0, p)),
                pl.BlockSpec((group_rows, LANES), lambda p, s: (0, 0)),
            ],
        ),
        out_shape=[
            jax.ShapeDtypeStruct((group_rows, q_cols), jnp.bfloat16),
            jax.ShapeDtypeStruct((group_rows, LANES), jnp.float32),
        ],
        name="attend",
    )(scalars, qkv, *keys)


def attend_back(k, scalars, qkv, grad, stat, keys, cos, sin, q_cols, group_rows):
    dp_size, portion = keys[0].shape[1], keys[0].shape[3]
    kv_heads = keys[0].shape[0]
    pairs = q_cols // LANES
    share = pairs // kv_heads
    keys_all = dp_size * portion
    whole = lambda p, s: (0, 0)
    table = pl.BlockSpec((group_rows, LANES), lambda p, s: (k, 0))
    kv_cols = 2 * kv_heads * HEAD_SIZE
    return pl.pallas_call(
        functools.partial(attend_back_kernel, share=share, kv_heads=kv_heads),
        grid_spec=pltpu.PrefetchScalarGridSpec(
            num_scalar_prefetch=1,
            grid=(pairs,),
            in_specs=[
                pl.BlockSpec((group_rows, LANES), lambda p, s: (k, p)),
                pl.BlockSpec((group_rows, LANES), lambda p, s: (0, p)),
                pl.BlockSpec((group_rows, LANES), whole),
            ]
            + key_specs(k, dp_size, portion, share)
            + [table, table],
            out_specs=[
                pl.BlockSpec((group_rows, LANES), lambda p, s: (0, p)),
                pl.BlockSpec((keys_all, kv_cols), whole),
                pl.BlockSpec((CONT, kv_cols), whole),
            ],
            scratch_shapes=[
                pltpu.VMEM((n, LANES), jnp.float32) for n in (keys_all, keys_all, CONT, CONT)
            ],
        ),
        out_shape=[
            jax.ShapeDtypeStruct((group_rows, q_cols), jnp.bfloat16),
            jax.ShapeDtypeStruct((keys_all, kv_cols), jnp.bfloat16),
            jax.ShapeDtypeStruct((CONT, kv_cols), jnp.float32),
        ],
        name="attend_back",
    )(scalars, qkv, grad, stat, *keys, cos, sin)


FF_PARTS = 1


def local(
    tokens,
    cotangent,
    prompt_len,
    cont_len,
    w_query,
    key_weight,
    value_weight,
    w_out,
    w_gate,
    w_up,
    w_down,
    attn_gain,
    ffn_gain,
):
    portion = PROMPT_DEV
    group_rows = PROMPT_DEV + CONT
    dp_size = lax.axis_size("dp")
    prompt_rows = PROMPT_DEV * dp_size
    dp_index = lax.axis_index("dp")
    tensor_index = lax.axis_index("tensor")
    relative = lax.axis_size("tensor") == NG
    local_rows = tokens.shape[0]
    q_cols = w_query.shape[1]
    kv_cols = key_weight.shape[1]
    head_count = q_cols // HEAD_SIZE
    group_count = kv_cols // HEAD_SIZE
    repeat = head_count // group_count
    qkv_cols = q_cols + 2 * kv_cols
    ff_cols = w_gate.shape[1]
    part = ff_cols // FF_PARTS

    attn_pack = gather_dp(
        jnp.concatenate([w_query, key_weight, value_weight, w_out.T], axis=1)
    )
    full_qkv = attn_pack[:, :qkv_cols]
    full_out_t = attn_pack[:, qkv_cols:]
    down_t = w_down.T
    gate_parts, up_parts, down_parts = [], [], []
    for c in range(FF_PARTS):
        cols = slice(c * part, (c + 1) * part)
        gate_parts.append(gather_dp(w_gate[:, cols]))
        up_parts.append(gather_dp(w_up[:, cols]))
        down_parts.append(gather_dp(down_t[:, cols]))
    gains = gather_dp(jnp.stack([attn_gain, ffn_gain], axis=1)).astype(jnp.float32)
    gain_one = gains[:, 0]
    gain_two = gains[:, 1]

    order = [tensor_index ^ k if relative else k for k in range(NG)]
    lengths = jnp.stack([prompt_len[g] for g in order]) if relative else prompt_len
    col_ids = jnp.arange(group_rows)[None, :]
    starts = lengths[:, None]
    positions = jnp.where(
        col_ids < portion, dp_index * portion + col_ids, starts + col_ids - portion
    ).reshape(-1)
    valid_rows = jnp.where(
        col_ids < portion,
        dp_index * portion + col_ids < prompt_len[:, None],
        col_ids - portion < cont_len,
    ).reshape(-1)
    valid_local = lax.dynamic_slice_in_dim(
        valid_rows.astype(jnp.float32), tensor_index * local_rows, local_rows
    )
    cosine_table, sine_values = (
        jnp.tile(table, (1, LANES // HEAD_SIZE)) for table in rope_tables(positions, HEAD_SIZE)
    )

    resid_in = tokens.astype(jnp.float32)
    unit_one, scale_one = norm_parts(resid_in)
    token_rows = jnp.concatenate(gather_blocks(tokens), axis=0).astype(jnp.float32)
    grad_y = cotangent.astype(jnp.float32) * valid_local[:, None]
    grad_ffn_blocks = gather_blocks(
        tie((RESID_SCALE * grad_y).astype(jnp.bfloat16), token_rows)
    )

    normed = (norm_parts(token_rows)[0] * gain_one).astype(jnp.bfloat16)
    qkv = rope(
        project(normed, full_qkv), cosine_table, sine_values, q_cols + kv_cols, group_rows
    )
    kv_grp = qkv[:, q_cols:].reshape(NG, group_rows, 2 * kv_cols)
    prompt_kv = gather_prompt(kv_grp[:, :portion])
    own_kv = kv_grp[:, portion:]

    def twice(array, first_col):
        heads = []
        for j in range(group_count):
            at = first_col + j * HEAD_SIZE
            one = array[..., at : at + HEAD_SIZE]
            heads.append(jnp.concatenate([one, one], axis=-1))
        return jnp.stack(heads)

    keys = [
        twice(prompt_kv, 0),
        twice(prompt_kv, kv_cols),
        twice(own_kv, 0),
        twice(own_kv, kv_cols),
    ]
    key_shift = dp_index * portion if dp_size == FAST_DP else 0
    scalars = [
        jnp.stack([dp_index * portion, lengths[k], jnp.int32(key_shift)]) for k in range(NG)
    ]
    scalars[2], grad_ffn_blocks = lax.optimization_barrier((scalars[2], grad_ffn_blocks))

    kept = {}

    def forward_group(k):
        mixed, stat = attend(k, scalars[k], qkv, keys, q_cols, group_rows)
        kept[k] = (stat, mixed)
        return dot_back(mixed, full_out_t)

    hidden = resid_in + RESID_SCALE * scatter_blocks(forward_group)
    unit_two, scale_two = norm_parts(hidden)
    normed_two = jnp.concatenate(
        gather_blocks((unit_two * gain_two).astype(jnp.bfloat16)), axis=0
    )
    grad_ffn = jnp.concatenate(grad_ffn_blocks, axis=0)

    products, grad_gates, grad_ups = [], [], []
    gate_grads, up_grads, down_grads = [], [], []
    for c in range(FF_PARTS):
        gate_val = project(normed_two, gate_parts[c])
        up_val = project(normed_two, up_parts[c])
        sigmoid_gate = jax.nn.sigmoid(gate_val)
        product = (gate_val * sigmoid_gate * up_val).astype(jnp.bfloat16)
        down_sum = dot_rows(grad_ffn, product).astype(jnp.bfloat16)
        down_grads.append(scatter_dp(down_sum))
        grad_prod = project(tie(grad_ffn, down_sum), down_parts[c])
        grad_gate_val = (
            grad_prod * up_val * sigmoid_gate * (1.0 + gate_val * (1.0 - sigmoid_gate))
        ).astype(jnp.bfloat16)
        grad_up_val = (grad_prod * gate_val * sigmoid_gate).astype(jnp.bfloat16)
        gate_sum = dot_rows(normed_two, grad_gate_val).astype(jnp.bfloat16)
        gate_grads.append(scatter_dp(gate_sum))
        up_sum = dot_rows(normed_two, grad_up_val).astype(jnp.bfloat16)
        up_grads.append(scatter_dp(up_sum))
        grad_gate_val, grad_up_val = tie((grad_gate_val, grad_up_val), gate_sum)
        products.append(product)
        grad_gates.append(grad_gate_val)
        grad_ups.append(grad_up_val)

    def rows_of(array, k):
        return array[k * group_rows : (k + 1) * group_rows]

    def ffn_back_block(k):
        total = 0.0
        for c in range(FF_PARTS):
            total = total + dot_back(rows_of(grad_gates[c], k), gate_parts[c])
            total = total + dot_back(rows_of(grad_ups[c], k), up_parts[c])
        return total

    def ffn_out_block(k):
        total = 0.0
        for c in range(FF_PARTS):
            total = total + dot_back(rows_of(products[c], k), down_parts[c])
        return total

    grad_normed_two = scatter_blocks(ffn_back_block)
    output = (hidden + RESID_SCALE * scatter_blocks(ffn_out_block)).astype(jnp.bfloat16)
    grad_hidden_norm, gain_two_part = norm_back(grad_normed_two, unit_two, scale_two, gain_two)
    grad_hidden = grad_y + grad_hidden_norm

    grad_attn_blocks = gather_blocks((RESID_SCALE * grad_hidden).astype(jnp.bfloat16))
    grad_attn = jnp.concatenate(grad_attn_blocks, axis=0)
    mixed_rows = jnp.concatenate([kept[k][1] for k in range(NG)], axis=0)
    out_sum = dot_rows(grad_attn, mixed_rows).astype(jnp.bfloat16)
    grad_out = scatter_dp(out_sum).T
    grad_attn_blocks[1:] = tie(grad_attn_blocks[1:], up_sum)
    grad_attn_blocks[1], down_grads = lax.optimization_barrier((grad_attn_blocks[1], down_grads))
    grad_attn_blocks[3], gate_grads = lax.optimization_barrier((grad_attn_blocks[3], gate_grads))

    backs = []
    for k in range(NG):
        grad_mixed = project(grad_attn_blocks[k], full_out_t).astype(jnp.bfloat16)
        backs.append(
            attend_back(
                k, scalars[k], qkv, grad_mixed, kept[k][0], keys,
                cosine_table, sine_values, q_cols, group_rows,
            )
        )
    kv_parts = []
    for pair in ((0, 1), (2, 3)):
        blocks = jnp.stack(
            [backs[k][1].reshape(dp_size, portion, 2 * kv_cols) for k in pair], axis=1
        )
        prompt_grad = scatter_prompt(blocks)
        for n, k in enumerate(pair):
            kv_parts += [prompt_grad[n], backs[k][2]]
    kv_grad = rope(
        jnp.concatenate(kv_parts, axis=0), cosine_table, -sine_values, kv_cols, group_rows
    )
    query_grad = jnp.concatenate([b[0] for b in backs], axis=0)
    qkv_grad = jnp.concatenate([query_grad, kv_grad], axis=1)
    qkv_sum = dot_rows(normed, qkv_grad).astype(jnp.bfloat16)
    qkv_w_grad = scatter_dp(qkv_sum)
    later_grad = tie(qkv_grad, qkv_sum)
    grad_normed = scatter_blocks(
        lambda k: dot_back(rows_of(qkv_grad if k == 3 else later_grad, k), full_qkv)
    )
    grad_input_norm, gain_one_part = norm_back(grad_normed, unit_one, scale_one, gain_one)
    input_grad = grad_hidden + grad_input_norm
    return (
        output,
        input_grad,
        qkv_w_grad[:, :q_cols],
        qkv_w_grad[:, q_cols : q_cols + kv_cols],
        qkv_w_grad[:, q_cols + kv_cols :],
        grad_out,
        jnp.concatenate(gate_grads, axis=1),
        jnp.concatenate(up_grads, axis=1),
        jnp.concatenate(down_grads, axis=1).T,
        scatter_gain(gain_one_part),
        scatter_gain(gain_two_part),
    )


def solution(mesh):
    placed = (
        P(("dp", "tensor"), None),
        P(("dp", "tensor"), None),
        P(),
        P(None, "dp"),
        P("dp", "tensor"),
        P("dp", "tensor"),
        P("dp", "tensor"),
        P("tensor", "dp"),
        P("dp", "tensor"),
        P("dp", "tensor"),
        P("tensor", "dp"),
        P("dp"),
        P("dp"),
    )
    return jax.shard_map(
        local,
        mesh=mesh,
        in_specs=placed,
        out_specs=(
            P(("dp", "tensor"), None),
            P(("dp", "tensor"), None),
            P("dp", "tensor"),
            P("dp", "tensor"),
            P("dp", "tensor"),
            P("tensor", "dp"),
            P("dp", "tensor"),
            P("dp", "tensor"),
            P("tensor", "dp"),
            P(("dp", "tensor")),
            P(("dp", "tensor")),
        ),
        check_vma=False,
    )
```
